128 devices in a mesh: rng: 8 (over z_lo, x), az: 16 (over y, z_hi, core).
Axes of the slice: x: 4, y: 4, z: 4 (z_hi: 2, z_lo: 2; z = z_hi * 2 + z_lo), core: 2. Of those that a mesh axis runs over, the one named last changes fastest.
Arguments:
- echoes: bfloat16 [16, 2, 64, 12288], P('az', None, None, 'rng'), may hold values from -6 to 6
- owner_map: int32 [8], replicated, may hold values from 0 to 15, as said below
- band_start: int32 [48, 16, 8], P('rng', 'az'), may hold values from 0 to 1536, as said below
- interp: bfloat16 [8, 16, 6144, 256], P(None, 'az', 'rng'), may hold values from -0.375 to 0.375
- steer_phase: float32 [8, 64, 16384], P(None, None, 'az'), may hold values from -3.140625 to 3.140625
Outputs:
- focused_image: bfloat16 [6144, 2, 16384], P('rng', None, 'az')
The draws below stay inside these ranges and needn't reach their ends.
Inputs may be any that keep to these rules, and one draw needn't show every extreme that they name: `owner_map`: the pings' slots are distinct. band_start[g, j, p] lies within 128 of (g mod 6) * 256 + 128.
All inputs are finite; a program needn't handle non-finite values.
Results may differ from the reference program's by a relative error of at most 0.01.
The reference program's roundings to bfloat16 on the way count: a program that leaves them out, or rounds other values in their place, can miss the bound.
Values may be sent and summed in bfloat16 or wider, within the bound.
No kernel may reach another device: no remote copies, remote signals or barrier semaphores. Data moves between devices by JAX's collectives and lax.ppermute only.
A program may use at most 128 MiB of HBM per device.

```python
import jax
import jax.numpy as jnp
from jax import lax

H = 64
PINGS = 8
BLK = 128
GUARD = 128
NBLK = 6
A_DEV = 1024
BAND = 256
S_DEV = 1536
NR = 6144
NA = 16384
NS = 12288
NBT = 48
N_RNG = 8
N_AZ = 16


def draw_owner_map(key, part):
    slots = NA // A_DEV
    first_key = jax.random.fold_in(key, 11)
    second_key = jax.random.fold_in(key, 12)
    inner = 1 + jax.random.permutation(first_key, slots - 2)[:PINGS - 2]
    values = jnp.concatenate([jnp.array([0, slots - 1], jnp.int32), inner.astype(jnp.int32)])
    order = jax.random.permutation(second_key, PINGS)
    return values[order].astype(jnp.int32)


def draw_band_start(key, part):
    slots = NA // A_DEV
    shift_key = jax.random.fold_in(key, 21)
    delay = jax.random.randint(shift_key, (NBT, slots, PINGS), -GUARD, GUARD + 1).astype(jnp.int32)
    delay = delay.at[0, 0, 0].set(-GUARD)
    delay = delay.at[NBT - 1, slots - 1, PINGS - 1].set(GUARD)
    nominal = jnp.arange(NBT).astype(jnp.int32) % NBLK * BAND + GUARD
    return (nominal[:, None, None] + delay).astype(jnp.int32)


def steps_of(rng, shape, pieces, smallest, top_value):
    factor_of, own = 1.0, jax.random.fold_in(rng, 6)
    for dim, blocks in pieces:
        steps = jnp.exp(jax.random.uniform(jax.random.fold_in(own, dim), (blocks,), jnp.float32, smallest / len(pieces), top_value / len(pieces)))
        factor_of = factor_of * jnp.repeat(steps, shape[dim] // blocks).reshape([-1 if axis == dim else 1 for axis in range(len(shape))])
    return factor_of


def centred(stream_key, dims, scale, most, pieces=(), kind=jnp.bfloat16):
    entries = jax.random.normal(stream_key, dims, jnp.float32) * scale
    if len(pieces) > 0:
        entries = steps_of(stream_key, dims, pieces, -0.22, 0.18) * entries
    return jnp.clip(entries, min=-most, max=most).astype(kind)


def setup_inputs(seed: int = 0) -> dict:
    keys = jax.random.split(jax.random.key(seed), 6)
    return {
        "echoes": centred(keys[0], (N_AZ, 2, H, NS), 1.0, 6.0, ((0, 16), (3, 8))),
        "owner_map": draw_owner_map(jax.random.fold_in(keys[5], 71), 0),
        "band_start": draw_band_start(jax.random.fold_in(keys[5], 71), 0),
        "interp": centred(keys[3], (PINGS, N_AZ, NR, BAND), BAND ** -0.5, 0.375, ((1, 16), (2, 8))),
        "steer_phase": jnp.clip(jax.random.uniform(keys[4], (PINGS, H, NA), jnp.float32, -3.140625, 3.140625), -3.140625, 3.140625),
    }


def autofocus_pass(image):
    blocks = image.reshape(N_RNG, NR // N_RNG, 2, NA)

    def sums(block):
        real_part = block[:, 0].astype(jnp.float32)
        imag_part = block[:, 1].astype(jnp.float32)
        cross = lax.optimization_barrier(jnp.sum(real_part[:, :-1] * imag_part[:, 1:] - imag_part[:, :-1] * real_part[:, 1:], axis=0))
        cross = jnp.concatenate([cross, jnp.zeros((1,), jnp.float32)])
        power = lax.optimization_barrier(jnp.sum(real_part * real_part + imag_part * imag_part, axis=0))
        return (cross, power)
    cross, power = lax.map(sums, blocks)
    cross = lax.optimization_barrier(jnp.sum(cross, axis=0))
    power = lax.optimization_barrier(jnp.sum(power, axis=0))
    slope = cross / (power + 1e-06)
    phase = jnp.cumsum(slope) - slope
    cosine = jnp.cos(phase)
    sine = jnp.sin(phase)

    def correct(block):
        real_part = block[:, 0].astype(jnp.float32)
        imag_part = block[:, 1].astype(jnp.float32)
        return jnp.stack([real_part * cosine + imag_part * sine, imag_part * cosine - real_part * sine], axis=1).astype(jnp.bfloat16)
    return lax.map(correct, blocks).reshape(NR, 2, NA)

def reference(echoes, owner_map, band_start, interp, steer_phase):
    padded = jnp.pad(echoes, ((0, 0), (0, 0), (0, 0), (GUARD, GUARD)))
    windows = padded[owner_map]
    scale = 1.0 / jnp.sqrt(jnp.float32(PINGS * H))
    tile_of_block = (jnp.arange(NBT) // NBLK).astype(jnp.int32)

    def one_tile(column):
        starts = lax.dynamic_slice_in_dim(band_start, column, 1, 1)[:, 0, :]
        offsets = tile_of_block[:, None] * S_DEV + starts

        def cut(window, start):
            return lax.dynamic_slice_in_dim(window, start, BAND, 2)
        slabs = jax.vmap(jax.vmap(cut, (0, 0)), (None, 0))(windows, offsets)
        kernels = lax.dynamic_slice_in_dim(interp, column, 1, 1)[:, 0].reshape(PINGS, NBT, BLK, BAND)
        focused = jnp.einsum('pgik,gpchk->gipch', kernels.astype(jnp.float32), slabs.astype(jnp.float32))
        focused = focused.astype(jnp.bfloat16).reshape(NR, PINGS * 2 * H)
        phases = lax.dynamic_slice_in_dim(steer_phase, column * A_DEV, A_DEV, 2)
        steer_re = (jnp.cos(phases) * scale).astype(jnp.bfloat16)
        steer_im = (jnp.sin(phases) * scale).astype(jnp.bfloat16)
        upper = jnp.stack([steer_re, steer_im], axis=2)
        lower = jnp.stack([-steer_im, steer_re], axis=2)
        steering = jnp.stack([upper, lower], axis=1).reshape(PINGS * 2 * H, 2 * A_DEV)
        return jnp.dot(focused, steering, preferred_element_type=jnp.float32).astype(jnp.bfloat16)
    tiles = lax.map(one_tile, jnp.arange(N_AZ).astype(jnp.int32))
    image0 = jnp.transpose(tiles.reshape(N_AZ, NR, 2, A_DEV), (1, 2, 0, 3)).reshape(NR, 2, NA)
    image1 = autofocus_pass(image0)
    return autofocus_pass(image1)
```

```python
import jax
import jax.numpy as jnp
from jax import lax
from jax.experimental import pallas as pl
from jax.experimental.pallas import tpu as pltpu
from jax.sharding import PartitionSpec as P

GUARD = 128
LANES = 128
N_Y, N_ZH, N_CORE = 4, 2, 2

PIO2_HI = 1.5707964
PIO2_LO = -4.371139e-8


def sine_cosine(x):
    turns = jnp.round(x * 0.63661975)
    r = (x - turns * PIO2_HI) - turns * PIO2_LO
    r2 = r * r
    sine = r + r * r2 * (-1.6666654611e-1 + r2 * (8.3321608736e-3 + r2 * -1.9515295891e-4))
    cosine = 1.0 - 0.5 * r2 + r2 * r2 * (
        4.166664568298827e-2 + r2 * (-1.388731625493765e-3 + r2 * 2.443315711809948e-5)
    )
    quadrant = turns.astype(jnp.int32)
    odd = (quadrant & 1) == 1
    first = jnp.where(odd, cosine, sine)
    second = jnp.where(odd, sine, cosine)
    sine = jnp.where((quadrant & 2) == 2, -first, first)
    cosine = jnp.where(((quadrant + 1) & 2) == 2, -second, second)
    return sine, cosine


def steering_kernel(scale, phase_ref, re_ref, im_ref):
    hydrophones = phase_ref.shape[1]
    sine, cosine = sine_cosine(phase_ref[0])
    steer_re = (cosine * scale).astype(jnp.bfloat16)
    steer_im = (sine * scale).astype(jnp.bfloat16)
    re_ref[:hydrophones] = steer_re
    re_ref[hydrophones:] = -steer_im
    im_ref[:hydrophones] = steer_im
    im_ref[hydrophones:] = steer_re


def steering(phases):
    pings, hydrophones, cells = phases.shape
    scale = float(1.0 / (pings * hydrophones) ** 0.5)
    block = pl.BlockSpec((2 * hydrophones, cells), lambda p: (p, 0))
    out = jax.ShapeDtypeStruct((pings * 2 * hydrophones, cells), jnp.bfloat16)
    return pl.pallas_call(
        lambda *refs: steering_kernel(scale, *refs),
        grid=(pings,),
        in_specs=[pl.BlockSpec((1, hydrophones, cells), lambda p: (p, 0, 0))],
        out_specs=[block, block],
        out_shape=[out, out],
        name="steering",
    )(phases)


def focus_kernel(n_slots, band, rel_ref, start_ref, *refs):
    slots = refs[:n_slots]
    interp_ref, re_ref, im_ref, out_ref, edge_ref, window, sems = refs[n_slots:]
    pings = window.shape[0]
    rows = window.shape[1]
    width = slots[0].shape[1]
    blocks = start_ref.shape[0] // pings
    cells = interp_ref.shape[1] // blocks
    p = pl.program_id(0)

    @pl.when(p == 0)
    def _():
        for ping in range(pings):
            for s in range(n_slots):

                @pl.when(rel_ref[ping] == s)
                def _():
                    pltpu.make_async_copy(
                        slots[s], window.at[ping, :, pl.ds(0, width)], sems.at[ping]
                    ).start()

    pltpu.make_async_copy(slots[0], window.at[p, :, pl.ds(0, width)], sems.at[p]).wait()
    for b in range(blocks):
        start = start_ref[b * pings + p]
        aligned = pl.multiple_of((start // LANES) * LANES, LANES)
        wide = window[p, :, pl.ds(aligned, band + LANES)].astype(jnp.float32)
        shift = (band + LANES) - (start - aligned)
        slab = pltpu.roll(wide, shift, 1)[:, :band].astype(jnp.bfloat16)
        kernel = interp_ref[0, b * cells : (b + 1) * cells, :]
        got = lax.dot_general(
            kernel, slab, (((1,), (1,)), ((), ())), preferred_element_type=jnp.float32
        )
        out_ref[b * cells : (b + 1) * cells, pl.ds(pl.multiple_of(p * rows, LANES), rows)] = (
            got.astype(jnp.bfloat16)
        )

    @pl.when(p == pings - 1)
    def _():
        n = re_ref.shape[1]
        focused = out_ref[...]

        def line(column_ref, low, row):
            part = column_ref[:, low : low + LANES]
            got = lax.dot_general(
                part, focused, (((0,), (1,)), ((), ())), preferred_element_type=jnp.float32
            )
            return got[row : row + 1, :].astype(jnp.bfloat16).astype(jnp.float32)

        edge_ref[0:1, :] = line(re_ref, 0, 0)
        edge_ref[1:2, :] = line(im_ref, 0, 0)
        edge_ref[2:3, :] = line(re_ref, n - LANES, LANES - 1)
        edge_ref[3:4, :] = line(im_ref, n - LANES, LANES - 1)


def focus(slots, rel, starts, interp, steer_re, steer_im):
    pings, range_cells, band = interp.shape
    rows, width = slots[0].shape
    any_spec = pl.BlockSpec(memory_space=pl.ANY)
    whole = pl.BlockSpec(steer_re.shape, lambda p, *_: (0, 0))
    kernel = lambda *refs: focus_kernel(len(slots), band, *refs)
    return pl.pallas_call(
        kernel,
        grid_spec=pltpu.PrefetchScalarGridSpec(
            num_scalar_prefetch=2,
            grid=(pings,),
            in_specs=[any_spec] * len(slots)
            + [pl.BlockSpec((1, range_cells, band), lambda p, *_: (p, 0, 0)), whole, whole],
            out_specs=[
                pl.BlockSpec((range_cells, pings * rows), lambda p, *_: (0, 0)),
                pl.BlockSpec((8, range_cells), lambda p, *_: (0, 0)),
            ],
            scratch_shapes=[
                pltpu.VMEM((pings, rows, width + LANES), jnp.bfloat16),
                pltpu.SemaphoreType.DMA((pings,)),
            ],
        ),
        out_shape=[
            jax.ShapeDtypeStruct((range_cells, pings * rows), jnp.bfloat16),
            jax.ShapeDtypeStruct((8, range_cells), jnp.float32),
        ],
        name="focus",
    )(rel, starts, *slots, interp, steer_re, steer_im)


def image_kernel(focused_ref, re_ref, im_ref, out_re, out_im, stats_ref):
    tile = 256
    rows, cells = out_re.shape
    focused = focused_ref[...]
    for n in range(cells // tile):
        part = slice(n * tile, (n + 1) * tile)
        out_re[:, part] = jnp.dot(
            focused, re_ref[:, part], preferred_element_type=jnp.float32
        ).astype(jnp.bfloat16)
        out_im[:, part] = jnp.dot(
            focused, im_ref[:, part], preferred_element_type=jnp.float32
        ).astype(jnp.bfloat16)
    step = 16
    half = 512

    def fold(x):
        return x[:8] + x[8:]

    stats_ref[...] = jnp.zeros_like(stats_ref)
    for low in range(0, cells, half):
        last = low + half == cells
        span = half if last else half + LANES

        def body(i, carry):
            power, real, imag = carry
            here = pl.ds(pl.multiple_of(i * step, step), step)
            a = out_re[here, low : low + span].astype(jnp.float32)
            b = out_im[here, low : low + span].astype(jnp.float32)
            na = pltpu.roll(a, span - 1, 1)[:, :half]
            nb = pltpu.roll(b, span - 1, 1)[:, :half]
            a, b = a[:, :half], b[:, :half]
            power = power + fold(a * a + b * b)
            real = real + fold(a * na + b * nb)
            imag = imag + fold(a * nb - b * na)
            return power, real, imag

        zero = jnp.zeros((8, half), jnp.float32)
        sums = lax.fori_loop(0, rows // step, body, (zero, zero, zero))
        for k, value in enumerate(sums):
            stats_ref[k : k + 1, low : low + half] = jnp.sum(value, axis=0, keepdims=True)


def image(focused, steer_re, steer_im):
    rows, cells = focused.shape[0], steer_re.shape[1]
    out = jax.ShapeDtypeStruct((rows, cells), jnp.bfloat16)
    return pl.pallas_call(
        image_kernel,
        out_shape=[out, out, jax.ShapeDtypeStruct((8, cells), jnp.float32)],
        name="image",
    )(focused, steer_re, steer_im)


def apply_kernel(re_ref, im_ref, cos_ref, sin_ref, out_ref, scratch):
    rows = re_ref.shape[0]
    tiles = re_ref.shape[1] // LANES
    for t in range(tiles):
        part = slice(t * LANES, (t + 1) * LANES)
        a = re_ref[:, part].astype(jnp.float32)
        b = im_ref[:, part].astype(jnp.float32)
        cosine = cos_ref[:, part]
        sine = sin_ref[:, part]
        scratch[pl.ds(2 * t, rows, stride=2 * tiles), :] = a * cosine + b * sine
        scratch[pl.ds(2 * t + 1, rows, stride=2 * tiles), :] = b * cosine - a * sine
    out_ref[...] = scratch[...].astype(jnp.bfloat16)


def apply(real, imag, cosine, sine):
    rows, cells = real.shape
    tiles = cells // LANES
    step = 64
    block = pl.BlockSpec((step, cells), lambda i: (i, 0))
    table = pl.BlockSpec((1, cells), lambda i: (0, 0))
    out = pl.pallas_call(
        apply_kernel,
        grid=(rows // step,),
        in_specs=[block, block, table, table],
        out_specs=pl.BlockSpec((step * 2 * tiles, LANES), lambda i: (i, 0)),
        out_shape=jax.ShapeDtypeStruct((rows * 2 * tiles, LANES), jnp.bfloat16),
        scratch_shapes=[pltpu.VMEM((step * 2 * tiles, LANES), jnp.float32)],
        name="apply",
    )(real, imag, cosine, sine)
    out = out.reshape(rows, tiles, 2, LANES).transpose(0, 2, 1, 3)
    return out.reshape(rows, 2, cells)


def send(x, axis, move):
    n = lax.axis_size(axis)
    return lax.ppermute(x, axis, [(i, move(i)) for i in range(n)])


def padded(block):
    n = lax.axis_size("rng")
    forward = [(i, i + 1) for i in range(n - 1)]
    backward = [(i + 1, i) for i in range(n - 1)]
    width = block.shape[1]
    low = lax.ppermute(block[:, width - GUARD :], "rng", forward)
    high = lax.ppermute(block[:, :GUARD], "rng", backward)
    return jnp.concatenate([low, block, high], axis=1)


def spread(own):
    up = lambda i: (i + 4) % 16
    down = lambda i: (i - 4) % 16
    across = lambda i: i ^ 2
    other = send(own, "az", across)
    slots = {(0, 0): own, (0, 1): other}
    for z, x in ((0, own), (1, other)):
        slots[3, z] = send(x, "az", up)
        slots[1, z] = send(x, "az", down)
    slots[2, 0] = send(slots[3, 0], "az", up)
    slots[2, 1] = send(slots[1, 1], "az", down)
    out = []
    for y in range(N_Y):
        for z in range(N_ZH):
            out.append(slots[y, z])
            out.append(send(slots[y, z], "az", lambda i: i ^ 1))
    return out


def per_device(echoes, owner_map, band_start, interp, steer_phase):
    hydrophones = echoes.shape[2]
    samples = echoes.shape[3]
    slots = spread(padded(echoes[0].reshape(2 * hydrophones, samples)))
    me = lax.axis_index("az")
    rel = (
        (owner_map // 4 - me // 4) % N_Y * 4
        + ((owner_map // 2) % 2 ^ (me // 2) % 2) * 2
        + (owner_map % 2 ^ me % 2)
    ).astype(jnp.int32)
    steer_re, steer_im = steering(steer_phase)
    focused, edges = focus(
        slots, rel, band_start.reshape(-1), interp[:, 0], steer_re, steer_im
    )
    n_az = lax.axis_size("az")
    halo = lax.ppermute(edges[:2], "az", [(i + 1, i) for i in range(n_az - 1)])
    real, imag, stats = image(focused, steer_re, steer_im)
    last_re, last_im = edges[2], edges[3]
    seam_re = jnp.sum(last_re * halo[0] + last_im * halo[1])
    seam_im = jnp.sum(last_re * halo[1] - last_im * halo[0])
    cells = real.shape[1]
    seam = jnp.stack([jnp.float32(0), seam_re, seam_im])[:, None]
    at_seam = (jnp.arange(cells) == cells - 1)[None, :]
    at_sum = (jnp.arange(3) == 0)[:, None]
    stats = jnp.where(at_seam & ~at_sum, seam, stats[:3])
    for mask in (1, 3, 4):
        stats = stats + send(stats, "rng", lambda i: i ^ mask)
    power, cross_re, cross_im = stats[0] + 1e-06, stats[1], stats[2]
    first = cross_im / power
    second = (cross_im * jnp.cos(first) - cross_re * jnp.sin(first)) / power
    slope = first + second
    summed = jnp.cumsum(slope)
    total = summed[-1:]
    before = jnp.zeros_like(total)
    for mask, bit in ((1, 1), (2, 2), (4, 4), (12, 8)):
        got = send(total, "az", lambda i: i ^ mask)
        before = before + jnp.where((me & bit) != 0, got, 0.0)
        total = total + got
    phase = (before + (summed - slope))[None, :]
    return apply(real, imag, jnp.cos(phase), jnp.sin(phase))


def solution(mesh):
    in_specs = (
        P("az", None, None, "rng"),
        P(),
        P("rng", "az", None),
        P(None, "az", "rng", None),
        P(None, None, "az"),
    )
    out_specs = P("rng", None, "az")
    return jax.shard_map(
        per_device, mesh=mesh, in_specs=in_specs, out_specs=out_specs, check_vma=False
    )
```

```python
import jax
import jax.numpy as jnp
from jax import lax
from jax.experimental import pallas as pl
from jax.experimental.pallas import tpu as pltpu
from jax.sharding import PartitionSpec as P


GUARD = 128
LANES = 128
VMEM = pl.BlockSpec(memory_space=pltpu.VMEM)
SMEM = pl.BlockSpec(memory_space=pltpu.SMEM)
HBM = pl.BlockSpec(memory_space=pltpu.HBM)

PIO2_HI = 1.5707964
PIO2_LO = -4.371139e-8


def sine_cosine(x):
    turns = jnp.round(x * 0.63661975)
    r = (x - turns * PIO2_HI) - turns * PIO2_LO
    r2 = r * r
    sine = r + r * r2 * (-1.6666654611e-1 + r2 * (8.3321608736e-3 + r2 * -1.9515295891e-4))
    cosine = 1.0 - 0.5 * r2 + r2 * r2 * (
        4.166664568298827e-2 + r2 * (-1.388731625493765e-3 + r2 * 2.443315711809948e-5)
    )
    quadrant = turns.astype(jnp.int32)
    odd = (quadrant & 1) == 1
    first = jnp.where(odd, cosine, sine)
    second = jnp.where(odd, sine, cosine)
    sine = jnp.where((quadrant & 2) == 2, -first, first)
    cosine = jnp.where(((quadrant + 1) & 2) == 2, -second, second)
    return sine, cosine


def kernel_call(body, out_shape, *args, scalars=0, vmem_mib=8):
    return pl.pallas_call(
        body,
        in_specs=[SMEM] * scalars + [VMEM] * (len(args) - scalars),
        out_specs=[VMEM] * len(out_shape),
        out_shape=out_shape,
        compiler_params=pltpu.CompilerParams(vmem_limit_bytes=vmem_mib << 20),
    )(*args)


def steering_kernel(scale, phase_hbm, re_hbm, im_hbm, edge_hbm, phases, re_ref, im_ref, edge_ref, sems, done):
    pings, hydrophones, cells = phases.shape
    rows = 2 * hydrophones
    for p in range(pings):
        pltpu.make_async_copy(phase_hbm.at[p], phases.at[p], sems.at[p]).start()
    lane = lax.broadcasted_iota(jnp.int32, (rows, LANES), 1)
    for p in range(pings):
        pltpu.make_async_copy(phase_hbm.at[p], phases.at[p], sems.at[p]).wait()
        here = pl.ds(rows * p, rows)
        upper = pl.ds(rows * p, hydrophones)
        lower = pl.ds(rows * p + hydrophones, hydrophones)
        sine, cosine = sine_cosine(phases[p])
        steer_re = (cosine * scale).astype(jnp.bfloat16)
        steer_im = (sine * scale).astype(jnp.bfloat16)
        re_ref[upper] = steer_re
        re_ref[lower] = -steer_im
        im_ref[upper] = steer_im
        im_ref[lower] = steer_re
        pltpu.make_async_copy(re_ref.at[here], re_hbm.at[here], done.at[0]).start()
        pltpu.make_async_copy(im_ref.at[here], im_hbm.at[here], done.at[1]).start()
    for p in range(pings):
        here = pl.ds(rows * p, rows)
        first_re = re_ref[here, :LANES].astype(jnp.float32)
        first_im = pltpu.roll(im_ref[here, :LANES].astype(jnp.float32), 1, 1)
        last_re = pltpu.roll(re_ref[here, cells - LANES :].astype(jnp.float32), LANES - 1, 1)
        last_im = im_ref[here, cells - LANES :].astype(jnp.float32)
        mixed = jnp.where(
            lane < 64,
            jnp.where(lane == 0, first_re, first_im),
            jnp.where(lane == LANES - 1, last_im, last_re),
        )
        edge_ref[:, here] = mixed.T.astype(jnp.bfloat16)
    edge_copy = pltpu.make_async_copy(edge_ref, edge_hbm, done.at[2])
    edge_copy.start()
    pltpu.make_async_copy(re_ref, re_hbm, done.at[0]).wait()
    pltpu.make_async_copy(im_ref, im_hbm, done.at[1]).wait()
    edge_copy.wait()


def steering(phases):
    pings, hydrophones, cells = phases.shape
    rows = pings * 2 * hydrophones
    scale = float(1.0 / (pings * hydrophones) ** 0.5)
    out = jax.ShapeDtypeStruct((rows, cells), jnp.bfloat16)
    edge = jax.ShapeDtypeStruct((LANES, rows), jnp.bfloat16)
    return pl.pallas_call(
        lambda *refs: steering_kernel(scale, *refs),
        in_specs=[HBM],
        out_specs=[HBM] * 3,
        out_shape=[pltpu.HBM(o.shape, o.dtype) for o in (out, out, edge)],
        scratch_shapes=[
            pltpu.VMEM(phases.shape, jnp.float32),
            pltpu.VMEM((rows, cells), jnp.bfloat16),
            pltpu.VMEM((rows, cells), jnp.bfloat16),
            pltpu.VMEM((LANES, rows), jnp.bfloat16),
            pltpu.SemaphoreType.DMA((pings,)),
            pltpu.SemaphoreType.DMA((3,)),
        ],
        compiler_params=pltpu.CompilerParams(vmem_limit_bytes=12 << 20),
        name="steering",
    )(pltpu.with_memory_space_constraint(phases, pltpu.HBM))


def focus_kernel(n_slots, place_ref, ping_ref, start_ref, *refs):
    slots = refs[:n_slots]
    ends = refs[n_slots : n_slots + n_slots // 2]
    interp_ref, weight_hbm, out_ref, edge_ref, window, weight_ref, sems = refs[
        n_slots + n_slots // 2 :
    ]
    pings, range_cells, band = interp_ref.shape
    rows, width = slots[0].shape
    blocks = start_ref.shape[0] // pings
    cells = range_cells // blocks
    span = band + LANES
    for s in range(n_slots):
        k = place_ref[s]
        end = ends[s // 4 * 2 + s % 2].at[s // 2 % 2]

        @pl.when(k >= 0)
        def _():
            for source, low in (
                (slots[s], GUARD),
                (end.at[:, pl.ds(0, GUARD)], 0),
                (end.at[:, pl.ds(GUARD, GUARD)], GUARD + width),
            ):
                part = window.at[k, :, pl.ds(low, source.shape[1])]
                pltpu.make_async_copy(source, part, sems.at[k]).start()

    weight_copy = pltpu.make_async_copy(weight_hbm, weight_ref, sems.at[pings])
    weight_copy.start()
    for k in range(pings):
        pltpu.make_async_copy(window.at[k], window.at[k], sems.at[k]).wait()
        p = ping_ref[k]
        column = pl.ds(pl.multiple_of(p * rows, LANES), rows)
        for b in range(blocks):
            start = start_ref[b * pings + p]
            aligned = jnp.minimum((start // LANES) * LANES, width + 2 * GUARD - span)
            aligned = pl.multiple_of(aligned, LANES)
            wide = window[k, :, pl.ds(aligned, span)]
            slab = pltpu.roll(wide, span - (start - aligned), 1)[:, :band]
            kernel = interp_ref[p, b * cells : (b + 1) * cells, :]
            got = lax.dot_general(
                kernel, slab, (((1,), (1,)), ((), ())), preferred_element_type=jnp.float32
            )
            out_ref[b * cells : (b + 1) * cells, column] = got.astype(jnp.bfloat16)

    weight_copy.wait()
    got = lax.dot_general(
        weight_ref[...], out_ref[...], (((1,), (1,)), ((), ())), preferred_element_type=jnp.float32
    )
    edge_ref[0:2, :] = got[0:2].astype(jnp.bfloat16).astype(jnp.float32)
    edge_ref[2:4, :] = got[LANES - 2 :].astype(jnp.bfloat16).astype(jnp.float32)


def focus(slots, ends, places, ping_at, starts, interp, edge_weights):
    pings, range_cells, _ = interp.shape
    rows, width = slots[0].shape
    call = pl.pallas_call(
        lambda *refs: focus_kernel(len(slots), *refs),
        in_specs=[SMEM] * 3 + [HBM] * (len(slots) + len(ends)) + [VMEM, HBM],
        out_specs=[VMEM] * 2,
        out_shape=[
            jax.ShapeDtypeStruct((range_cells, pings * rows), jnp.bfloat16),
            jax.ShapeDtypeStruct((4, range_cells), jnp.float32),
        ],
        scratch_shapes=[
            pltpu.VMEM((pings, rows, width + 2 * GUARD), jnp.bfloat16),
            pltpu.VMEM(edge_weights.shape, jnp.bfloat16),
            pltpu.SemaphoreType.DMA((pings + 1,)),
        ],
        compiler_params=pltpu.CompilerParams(vmem_limit_bytes=16 << 20),
        name="focus",
    )
    local = [pltpu.with_memory_space_constraint(x, pltpu.HBM) for x in (*slots, *ends)]
    edge_weights = pltpu.with_memory_space_constraint(edge_weights, pltpu.HBM)
    return call(places, ping_at, starts, *local, interp, edge_weights)


def image_kernel(focused_ref, re_ref, im_ref, out_re, out_im, stats_ref):
    tile = 512
    rows, cells = out_re.shape
    focused = focused_ref[...]
    for n in range(cells // tile):
        part = slice(n * tile, (n + 1) * tile)
        out_re[:, part] = jnp.dot(
            focused, re_ref[:, part], preferred_element_type=jnp.float32
        ).astype(jnp.bfloat16)
        out_im[:, part] = jnp.dot(
            focused, im_ref[:, part], preferred_element_type=jnp.float32
        ).astype(jnp.bfloat16)
    step = 16
    half = 512

    def fold(x):
        return x[:8] + x[8:]

    stats_ref[...] = jnp.zeros_like(stats_ref)
    for low in range(0, cells, half):
        last = low + half == cells
        span = half if last else half + LANES

        def body(i, carry):
            power, real, imag = carry
            here = pl.ds(pl.multiple_of(i * step, step), step)
            a = out_re[here, low : low + span].astype(jnp.float32)
            b = out_im[here, low : low + span].astype(jnp.float32)
            na = pltpu.roll(a, span - 1, 1)[:, :half]
            nb = pltpu.roll(b, span - 1, 1)[:, :half]
            a, b = a[:, :half], b[:, :half]
            power = power + fold(a * a + b * b)
            real = real + fold(a * na + b * nb)
            imag = imag + fold(a * nb - b * na)
            return power, real, imag

        zero = jnp.zeros((8, half), jnp.float32)
        sums = lax.fori_loop(0, rows // step, body, (zero, zero, zero), unroll=8)
        for k, value in enumerate(sums):
            stats_ref[k : k + 1, low : low + half] = jnp.sum(value, axis=0, keepdims=True)


def image(focused, steer_re, steer_im):
    rows, cells = focused.shape[0], steer_re.shape[1]
    out = jax.ShapeDtypeStruct((rows, cells), jnp.bfloat16)
    return kernel_call(
        image_kernel,
        [out, out, jax.ShapeDtypeStruct((8, cells), jnp.float32)],
        focused,
        steer_re,
        steer_im,
    )


def seam_kernel(stats_ref, edges_ref, halo_ref, out_ref):
    cells = stats_ref.shape[1]
    last_re, last_im = edges_ref[2:3, :], edges_ref[3:4, :]
    next_re, next_im = halo_ref[0:1, :], halo_ref[1:2, :]
    real = jnp.sum(last_re * next_re + last_im * next_im, axis=1, keepdims=True)
    imag = jnp.sum(last_re * next_im - last_im * next_re, axis=1, keepdims=True)
    at = lax.broadcasted_iota(jnp.int32, (1, cells), 1) == cells - 1
    out_ref[...] = stats_ref[...]
    out_ref[1:2, :] = jnp.where(at, real, stats_ref[1:2, :])
    out_ref[2:3, :] = jnp.where(at, imag, stats_ref[2:3, :])


def slope_kernel(stats_ref, more_ref, phase_ref, total_ref):
    cells = stats_ref.shape[1]
    stats = stats_ref[...] + more_ref[...]
    power, real, imag = stats[0:1] + 1e-06, stats[1:2], stats[2:3]
    first = imag / power
    second = (imag * jnp.cos(first) - real * jnp.sin(first)) / power
    slope = first + second
    lane = lax.broadcasted_iota(jnp.int32, (1, cells), 1)
    summed = slope
    step = 1
    while step < cells:
        summed = summed + jnp.where(lane >= step, pltpu.roll(summed, step, 1), 0.0)
        step *= 2
    phase_ref[...] = summed - slope
    total_ref[...] = jnp.broadcast_to(jnp.sum(slope, axis=1, keepdims=True), total_ref.shape)


def apply_kernel(re_ref, im_ref, phase_ref, before_ref, out_ref, scratch, cos_ref, sin_ref):
    step = scratch.shape[0] * LANES // (2 * re_ref.shape[1])
    tiles = re_ref.shape[1] // LANES

    @pl.when(pl.program_id(0) == 0)
    def _():
        phase = phase_ref[...] + before_ref[0:1, 0:1]
        cos_ref[...] = jnp.cos(phase)
        sin_ref[...] = jnp.sin(phase)

    here = pl.ds(pl.multiple_of(pl.program_id(0) * step, step), step)
    for t in range(tiles):
        part = slice(t * LANES, (t + 1) * LANES)
        a = re_ref[here, part].astype(jnp.float32)
        b = im_ref[here, part].astype(jnp.float32)
        cosine = cos_ref[:, part]
        sine = sin_ref[:, part]
        scratch[pl.ds(2 * t, step, stride=2 * tiles), :] = a * cosine + b * sine
        scratch[pl.ds(2 * t + 1, step, stride=2 * tiles), :] = b * cosine - a * sine
    out_ref[...] = scratch[...].astype(jnp.bfloat16)


def apply(real, imag, phase, before):
    rows, cells = real.shape
    tiles = cells // LANES
    step = 128
    out = pl.pallas_call(
        apply_kernel,
        grid=(rows // step,),
        in_specs=[VMEM] * 4,
        out_specs=pl.BlockSpec((step * 2 * tiles, LANES), lambda i: (i, 0)),
        out_shape=jax.ShapeDtypeStruct((rows * 2 * tiles, LANES), jnp.bfloat16),
        scratch_shapes=[
            pltpu.VMEM((step * 2 * tiles, LANES), jnp.float32),
            pltpu.VMEM((1, cells), jnp.float32),
            pltpu.VMEM((1, cells), jnp.float32),
        ],
        compiler_params=pltpu.CompilerParams(vmem_limit_bytes=12 << 20),
        name="apply",
    )(real, imag, phase, before)
    out = out.reshape(rows, tiles, 2, LANES).transpose(0, 2, 1, 3)
    return out.reshape(rows, 2, cells)


def send(x, axis, move):
    n = lax.axis_size(axis)
    return lax.ppermute(x, axis, [(i, move(i)) for i in range(n)])


def up(x):
    return send(x, "az", lambda i: (i + 4) % 16)


def down(x):
    return send(x, "az", lambda i: (i - 4) % 16)


def across(x):
    return send(x, "az", lambda i: i ^ 2)


def partner(x):
    return send(x, "az", lambda i: i ^ 1)


def spread(block):
    n = lax.axis_size("rng")
    width = block.shape[1]
    above, below, other = up(block), down(block), across(block)
    low = lax.ppermute(block[:, width - GUARD :], "rng", [(i, i + 1) for i in range(n - 1)])
    high = lax.ppermute(block[:, :GUARD], "rng", [(i + 1, i) for i in range(n - 1)])
    ends = jnp.concatenate([low, high], axis=1)
    passed = jnp.where(lax.axis_index("az") & 1 == 0, above, below)
    opposite = send(passed, "az", lambda i: (i + (4, -4)[i & 1]) % 16)
    slots = {(0, 0): block, (3, 0): above, (1, 0): below, (2, 0): opposite, (0, 1): other}
    slots[3, 1] = up(other)
    slots[1, 1] = down(other)
    slots[2, 1] = across(opposite)
    ends = jnp.stack([ends, across(ends)])
    far = send(ends, "az", lambda i: (i + 8) % 16)
    ends = [ends, down(ends), far, up(ends)]
    out_slots, out_ends = [], []
    for y in range(4):
        out_ends += [ends[y], partner(ends[y])]
        for z in range(2):
            out_slots += [slots[y, z], partner(slots[y, z])]
    return out_slots, out_ends


def per_device_body(echoes, owner_map, band_start, interp, steer_phase):
    hydrophones, samples = echoes.shape[2:]
    n_az = lax.axis_size("az")
    me = lax.axis_index("az")
    relative = ((((owner_map >> 2) - (me >> 2)) & 3) << 2) | ((owner_map ^ me) & 3)
    slot = jnp.arange(n_az, dtype=jnp.int32)
    place = jnp.sum(relative[None, :] < relative[:, None], axis=1).astype(jnp.int32)
    matches = relative[None, :] == slot[:, None]
    places = jnp.sum(jnp.where(matches, place[None, :] + 1, 0), axis=1) - 1
    number = jnp.arange(owner_map.shape[0], dtype=jnp.int32)
    ping_at = jnp.sum(jnp.where(place[None, :] == number[:, None], number[None, :], 0), axis=1)
    starts = band_start.reshape(-1)
    steer_re, steer_im, edge_weights = steering(steer_phase)
    slots, ends = spread(echoes[0].reshape(2 * hydrophones, samples))
    focused, edges = focus(
        slots, ends, places, ping_at, starts, interp[:, 0], edge_weights
    )
    halo = lax.ppermute(edges[:2], "az", [(i + 1, i) for i in range(n_az - 1)])
    real, imag, stats = image(focused, steer_re, steer_im)
    (stats,) = kernel_call(
        seam_kernel, [jax.ShapeDtypeStruct(stats.shape, jnp.float32)], stats, edges, halo,
    )
    for mask in (1, 3):
        stats = stats + send(stats, "rng", lambda i: i ^ mask)
    phase, total = kernel_call(
        slope_kernel,
        [
            jax.ShapeDtypeStruct((1, stats.shape[1]), jnp.float32),
            jax.ShapeDtypeStruct((8, LANES), jnp.float32),
        ],
        stats,
        send(stats, "rng", lambda i: i ^ 4),
    )
    before = jnp.zeros_like(total)
    for mask, bit in ((1, 1), (2, 2), (4, 4), (12, 8)):
        got = send(total, "az", lambda i: i ^ mask)
        before = before + jnp.where((me & bit) != 0, got, 0.0)
        total = total + got
    return apply(real, imag, phase, before)


def solution(mesh):
    in_specs = (
        P("az", None, None, "rng"),
        P(),
        P("rng", "az", None),
        P(None, "az", "rng", None),
        P(None, None, "az"),
    )
    out_specs = P("rng", None, "az")
    return jax.shard_map(
        per_device_body, mesh=mesh, in_specs=in_specs, out_specs=out_specs, check_vma=False
    )
```

```python
import jax
import jax.numpy as jnp
from jax import lax
from jax.experimental import pallas as pl
from jax.experimental.pallas import tpu as pltpu
from jax.sharding import PartitionSpec as P


GUARD = 128
LANES = 128
VMEM = pl.BlockSpec(memory_space=pltpu.VMEM)
SMEM = pl.BlockSpec(memory_space=pltpu.SMEM)
HBM = pl.BlockSpec(memory_space=pltpu.HBM)
ANY = pl.BlockSpec(memory_space=pl.ANY)

PIO2_HI = 1.5707964
PIO2_LO = -4.371139e-8


def sine_cosine(x):
    turns = jnp.round(x * 0.63661975)
    r = (x - turns * PIO2_HI) - turns * PIO2_LO
    r2 = r * r
    sine = r + r * r2 * (-1.6666654611e-1 + r2 * (8.3321608736e-3 + r2 * -1.9515295891e-4))
    cosine = 1.0 - 0.5 * r2 + r2 * r2 * (
        4.166664568298827e-2 + r2 * (-1.388731625493765e-3 + r2 * 2.443315711809948e-5)
    )
    quadrant = turns.astype(jnp.int32)
    odd = (quadrant & 1) == 1
    first = jnp.where(odd, cosine, sine)
    second = jnp.where(odd, sine, cosine)
    sine = jnp.where((quadrant & 2) == 2, -first, first)
    cosine = jnp.where(((quadrant + 1) & 2) == 2, -second, second)
    return sine, cosine


def kernel_call(body, out_shape, *args, scalars=0, vmem_mib=8):
    return pl.pallas_call(
        body,
        in_specs=[SMEM] * scalars + [VMEM] * (len(args) - scalars),
        out_specs=[VMEM] * len(out_shape),
        out_shape=out_shape,
        compiler_params=pltpu.CompilerParams(vmem_limit_bytes=vmem_mib << 20),
    )(*args)


def steering_kernel(scale, phase_hbm, re_hbm, im_hbm, edge_hbm, phases, re_ref, im_ref, edge_ref, sems, done):
    pings, hydrophones, cells = phases.shape
    rows = 2 * hydrophones
    for p in range(pings):
        pltpu.make_async_copy(phase_hbm.at[p], phases.at[p], sems.at[p]).start()
    lane = lax.broadcasted_iota(jnp.int32, (rows, LANES), 1)
    for p in range(pings):
        pltpu.make_async_copy(phase_hbm.at[p], phases.at[p], sems.at[p]).wait()
        here = pl.ds(rows * p, rows)
        upper = pl.ds(rows * p, hydrophones)
        lower = pl.ds(rows * p + hydrophones, hydrophones)
        sine, cosine = sine_cosine(phases[p])
        steer_re = (cosine * scale).astype(jnp.bfloat16)
        steer_im = (sine * scale).astype(jnp.bfloat16)
        re_ref[upper] = steer_re
        re_ref[lower] = -steer_im
        im_ref[upper] = steer_im
        im_ref[lower] = steer_re
        pltpu.make_async_copy(re_ref.at[here], re_hbm.at[here], done.at[0]).start()
        pltpu.make_async_copy(im_ref.at[here], im_hbm.at[here], done.at[1]).start()
    for p in range(pings):
        here = pl.ds(rows * p, rows)
        first_re = re_ref[here, :LANES].astype(jnp.float32)
        first_im = pltpu.roll(im_ref[here, :LANES].astype(jnp.float32), 1, 1)
        last_re = pltpu.roll(re_ref[here, cells - LANES :].astype(jnp.float32), LANES - 1, 1)
        last_im = im_ref[here, cells - LANES :].astype(jnp.float32)
        mixed = jnp.where(
            lane < 64,
            jnp.where(lane == 0, first_re, first_im),
            jnp.where(lane == LANES - 1, last_im, last_re),
        )
        edge_ref[:, here] = mixed.T.astype(jnp.bfloat16)
    edge_copy = pltpu.make_async_copy(edge_ref, edge_hbm, done.at[2])
    edge_copy.start()
    pltpu.make_async_copy(re_ref, re_hbm, done.at[0]).wait()
    pltpu.make_async_copy(im_ref, im_hbm, done.at[1]).wait()
    edge_copy.wait()


def steering(phases):
    pings, hydrophones, cells = phases.shape
    rows = pings * 2 * hydrophones
    scale = float(1.0 / (pings * hydrophones) ** 0.5)
    out = jax.ShapeDtypeStruct((rows, cells), jnp.bfloat16)
    edge = jax.ShapeDtypeStruct((LANES, rows), jnp.bfloat16)
    return pl.pallas_call(
        lambda *refs: steering_kernel(scale, *refs),
        in_specs=[HBM],
        out_specs=[HBM] * 3,
        out_shape=[pltpu.HBM(o.shape, o.dtype) for o in (out, out, edge)],
        scratch_shapes=[
            pltpu.VMEM(phases.shape, jnp.float32),
            pltpu.VMEM((rows, cells), jnp.bfloat16),
            pltpu.VMEM((rows, cells), jnp.bfloat16),
            pltpu.VMEM((LANES, rows), jnp.bfloat16),
            pltpu.SemaphoreType.DMA((pings,)),
            pltpu.SemaphoreType.DMA((3,)),
        ],
        compiler_params=pltpu.CompilerParams(vmem_limit_bytes=12 << 20),
        name="steering",
    )(pltpu.with_memory_space_constraint(phases, pltpu.HBM))


def focus_kernel(n_slots, me_ref, owner_ref, start_ref, *refs):
    slots = refs[:n_slots]
    ends = refs[n_slots : n_slots + n_slots // 2]
    interp_ref, weight_hbm, out_ref, edge_ref, window, weight_ref, place_ref, ping_ref, sems = refs[
        n_slots + n_slots // 2 :
    ]
    me = me_ref[0]
    pings, range_cells, band = interp_ref.shape
    rows, width = slots[0].shape
    blocks = start_ref.shape[0]
    cells = range_cells // blocks
    span = band + LANES
    for s in range(n_slots):
        place_ref[s] = -1
    owners = [owner_ref[p] for p in range(pings)]
    relative = [((((o >> 2) - (me >> 2)) & 3) << 2) | ((o ^ me) & 3) for o in owners]
    for p in range(pings):
        k = sum((relative[q] < relative[p]).astype(jnp.int32) for q in range(pings) if q != p)
        place_ref[relative[p]] = k
        ping_ref[k] = p
    for s in range(n_slots):
        k = place_ref[s]
        end = ends[s // 4 * 2 + s % 2].at[s // 2 % 2]

        @pl.when(k >= 0)
        def _():
            for source, low in (
                (slots[s], GUARD),
                (end.at[:, pl.ds(0, GUARD)], 0),
                (end.at[:, pl.ds(GUARD, GUARD)], GUARD + width),
            ):
                part = window.at[k, :, pl.ds(low, source.shape[1])]
                pltpu.make_async_copy(source, part, sems.at[k]).start()

    weight_copy = pltpu.make_async_copy(weight_hbm, weight_ref, sems.at[pings])
    weight_copy.start()
    for k in range(pings):
        pltpu.make_async_copy(window.at[k], window.at[k], sems.at[k]).wait()
        p = ping_ref[k]
        column = pl.ds(pl.multiple_of(p * rows, LANES), rows)
        for b in range(blocks):
            start = start_ref[b, 0, p]
            aligned = jnp.minimum((start // LANES) * LANES, width + 2 * GUARD - span)
            aligned = pl.multiple_of(aligned, LANES)
            wide = window[k, :, pl.ds(aligned, span)]
            slab = pltpu.roll(wide, span - (start - aligned), 1)[:, :band]
            kernel = interp_ref[p, b * cells : (b + 1) * cells, :]
            got = lax.dot_general(
                kernel, slab, (((1,), (1,)), ((), ())), preferred_element_type=jnp.float32
            )
            out_ref[b * cells : (b + 1) * cells, column] = got.astype(jnp.bfloat16)

    weight_copy.wait()
    got = lax.dot_general(
        weight_ref[...], out_ref[...], (((1,), (1,)), ((), ())), preferred_element_type=jnp.float32
    )
    edge_ref[0:2, :] = got[0:2].astype(jnp.bfloat16).astype(jnp.float32)
    edge_ref[2:4, :] = got[LANES - 2 :].astype(jnp.bfloat16).astype(jnp.float32)


def focus(slots, ends, me, owner_map, starts, interp, edge_weights):
    pings, range_cells, _ = interp.shape
    rows, width = slots[0].shape
    call = pl.pallas_call(
        lambda *refs: focus_kernel(len(slots), *refs),
        in_specs=[SMEM] * 3 + [ANY] * (len(slots) + len(ends)) + [VMEM, HBM],
        out_specs=[VMEM] * 2,
        out_shape=[
            jax.ShapeDtypeStruct((range_cells, pings * rows), jnp.bfloat16),
            jax.ShapeDtypeStruct((4, range_cells), jnp.float32),
        ],
        scratch_shapes=[
            pltpu.VMEM((pings, rows, width + 2 * GUARD), jnp.bfloat16),
            pltpu.VMEM(edge_weights.shape, jnp.bfloat16),
            pltpu.SMEM((len(slots),), jnp.int32),
            pltpu.SMEM((pings,), jnp.int32),
            pltpu.SemaphoreType.DMA((pings + 1,)),
        ],
        compiler_params=pltpu.CompilerParams(vmem_limit_bytes=16 << 20),
        name="focus",
    )
    edge_weights = pltpu.with_memory_space_constraint(edge_weights, pltpu.HBM)
    return call(me, owner_map, starts, *slots, *ends, interp, edge_weights)


def image_kernel(focused_ref, re_ref, im_ref, out_re, out_im, stats_ref):
    tile = 512
    rows, cells = out_re.shape
    focused = focused_ref[...]
    for n in range(cells // tile):
        part = slice(n * tile, (n + 1) * tile)
        out_re[:, part] = jnp.dot(
            focused, re_ref[:, part], preferred_element_type=jnp.float32
        ).astype(jnp.bfloat16)
        out_im[:, part] = jnp.dot(
            focused, im_ref[:, part], preferred_element_type=jnp.float32
        ).astype(jnp.bfloat16)
    step = 16
    half = 512

    def fold(x):
        return x[:8] + x[8:]

    stats_ref[...] = jnp.zeros_like(stats_ref)
    for low in range(0, cells, half):
        last = low + half == cells
        span = half if last else half + LANES

        def body(i, carry):
            power, real, imag = carry
            here = pl.ds(pl.multiple_of(i * step, step), step)
            a = out_re[here, low : low + span].astype(jnp.float32)
            b = out_im[here, low : low + span].astype(jnp.float32)
            na = pltpu.roll(a, span - 1, 1)[:, :half]
            nb = pltpu.roll(b, span - 1, 1)[:, :half]
            a, b = a[:, :half], b[:, :half]
            power = power + fold(a * a + b * b)
            real = real + fold(a * na + b * nb)
            imag = imag + fold(a * nb - b * na)
            return power, real, imag

        zero = jnp.zeros((8, half), jnp.float32)
        sums = lax.fori_loop(0, rows // step, body, (zero, zero, zero), unroll=8)
        for k, value in enumerate(sums):
            stats_ref[k : k + 1, low : low + half] = jnp.sum(value, axis=0, keepdims=True)


def image(focused, steer_re, steer_im):
    rows, cells = focused.shape[0], steer_re.shape[1]
    out = jax.ShapeDtypeStruct((rows, cells), jnp.bfloat16)
    return kernel_call(
        image_kernel,
        [out, out, jax.ShapeDtypeStruct((4, cells), jnp.float32)],
        focused,
        steer_re,
        steer_im,
    )


def seam_kernel(stats_ref, edges_ref, halo_ref, out_ref):
    cells = stats_ref.shape[1]
    last_re, last_im = edges_ref[2:3, :], edges_ref[3:4, :]
    next_re, next_im = halo_ref[0:1, :], halo_ref[1:2, :]
    real = jnp.sum(last_re * next_re + last_im * next_im, axis=1, keepdims=True)
    imag = jnp.sum(last_re * next_im - last_im * next_re, axis=1, keepdims=True)
    at = lax.broadcasted_iota(jnp.int32, (1, cells), 1) == cells - 1
    out_ref[...] = stats_ref[...]
    out_ref[1:2, :] = jnp.where(at, real, stats_ref[1:2, :])
    out_ref[2:3, :] = jnp.where(at, imag, stats_ref[2:3, :])


def slope_kernel(stats_ref, more_ref, phase_ref, total_ref):
    cells = stats_ref.shape[1]
    stats = stats_ref[...] + more_ref[...]
    power, real, imag = stats[0:1] + 1e-06, stats[1:2], stats[2:3]
    first = imag / power
    second = (imag * jnp.cos(first) - real * jnp.sin(first)) / power
    slope = first + second
    lane = lax.broadcasted_iota(jnp.int32, (1, cells), 1)
    summed = slope
    step = 1
    while step < cells:
        summed = summed + jnp.where(lane >= step, pltpu.roll(summed, step, 1), 0.0)
        step *= 2
    phase_ref[...] = summed - slope
    total_ref[...] = jnp.broadcast_to(jnp.sum(slope, axis=1, keepdims=True), total_ref.shape)


def apply_kernel(re_ref, im_ref, phase_ref, before_ref, out_ref, scratch, cos_ref, sin_ref):
    tiles = re_ref.shape[1] // LANES
    step = out_ref.shape[0] // (2 * tiles)
    stride = scratch.shape[0] // step

    @pl.when(pl.program_id(0) == 0)
    def _():
        phase = phase_ref[...] + before_ref[0:1, 0:1]
        cos_ref[...] = jnp.cos(phase)
        sin_ref[...] = jnp.sin(phase)

    here = pl.ds(pl.multiple_of(pl.program_id(0) * step, step), step)
    for t in range(tiles):
        part = slice(t * LANES, (t + 1) * LANES)
        a = re_ref[here, part].astype(jnp.float32)
        b = im_ref[here, part].astype(jnp.float32)
        cosine = cos_ref[:, part]
        sine = sin_ref[:, part]
        scratch[pl.ds(2 * t, step, stride=stride), :] = a * cosine + b * sine
        scratch[pl.ds(2 * t + 1, step, stride=stride), :] = b * cosine - a * sine
    for r in range(step):
        cell = scratch[r * stride : r * stride + 2 * tiles, :]
        out_ref[2 * tiles * r : 2 * tiles * (r + 1), :] = cell.astype(jnp.bfloat16)


def apply(real, imag, phase, before):
    rows, cells = real.shape
    tiles = cells // LANES
    step = 128
    out = pl.pallas_call(
        apply_kernel,
        grid=(rows // step,),
        in_specs=[VMEM] * 4,
        out_specs=pl.BlockSpec((step * 2 * tiles, LANES), lambda i: (i, 0)),
        out_shape=jax.ShapeDtypeStruct((rows * 2 * tiles, LANES), jnp.bfloat16),
        scratch_shapes=[
            pltpu.VMEM((step * (2 * tiles + 2), LANES), jnp.float32),
            pltpu.VMEM((1, cells), jnp.float32),
            pltpu.VMEM((1, cells), jnp.float32),
        ],
        compiler_params=pltpu.CompilerParams(vmem_limit_bytes=12 << 20),
        name="apply",
    )(real, imag, phase, before)
    out = out.reshape(rows, tiles, 2, LANES).transpose(0, 2, 1, 3)
    return out.reshape(rows, 2, cells)


def send(x, axis, move):
    n = lax.axis_size(axis)
    return lax.ppermute(x, axis, [(i, move(i)) for i in range(n)])


def up(x):
    return send(x, "az", lambda i: (i + 4) % 16)


def down(x):
    return send(x, "az", lambda i: (i - 4) % 16)


def across(x):
    return send(x, "az", lambda i: i ^ 2)


def partner(x):
    return send(x, "az", lambda i: i ^ 1)


def join_kernel(low_ref, high_ref, out_ref):
    out_ref[:, :GUARD] = low_ref[...]
    out_ref[:, GUARD:] = high_ref[...]


def select_kernel(me_ref, above_ref, below_ref, out_ref):
    even = me_ref[0] & 1 == 0

    @pl.when(even)
    def _():
        out_ref[...] = above_ref[...]

    @pl.when(jnp.logical_not(even))
    def _():
        out_ref[...] = below_ref[...]


def spread(block):
    n = lax.axis_size("rng")
    width = block.shape[1]
    above, below, other = up(block), down(block), across(block)
    low = lax.ppermute(block[:, width - GUARD :], "rng", [(i, i + 1) for i in range(n - 1)])
    high = lax.ppermute(block[:, :GUARD], "rng", [(i + 1, i) for i in range(n - 1)])
    (ends,) = kernel_call(
        join_kernel, [jax.ShapeDtypeStruct((block.shape[0], 2 * GUARD), jnp.bfloat16)], low, high
    )
    (passed,) = kernel_call(
        select_kernel,
        [jax.ShapeDtypeStruct(block.shape, jnp.bfloat16)],
        lax.axis_index("az").reshape(1),
        above,
        below,
        scalars=1,
    )
    opposite = send(passed, "az", lambda i: (i + (4, -4)[i & 1]) % 16)
    slots = {(0, 0): block, (3, 0): above, (1, 0): below, (2, 0): opposite, (0, 1): other}
    slots[3, 1] = up(other)
    slots[1, 1] = down(other)
    slots[2, 1] = across(opposite)
    ends = jnp.stack([ends, across(ends)])
    far = send(ends, "az", lambda i: (i + 8) % 16)
    ends = [ends, down(ends), far, up(ends)]
    out_slots, out_ends = [], []
    for y in range(4):
        out_ends += [ends[y], partner(ends[y])]
        for z in range(2):
            out_slots += [slots[y, z], partner(slots[y, z])]
    return out_slots, out_ends


def per_device_body(echoes, owner_map, band_start, interp, steer_phase):
    hydrophones, samples = echoes.shape[2:]
    n_az = lax.axis_size("az")
    me = lax.axis_index("az")
    steer_re, steer_im, edge_weights = steering(steer_phase)
    slots, ends = spread(echoes[0].reshape(2 * hydrophones, samples))
    focused, edges = focus(
        slots, ends, me.reshape(1), owner_map, band_start, interp[:, 0], edge_weights
    )
    halo = lax.ppermute(edges[:2], "az", [(i + 1, i) for i in range(n_az - 1)])
    real, imag, stats = image(focused, steer_re, steer_im)
    (stats,) = kernel_call(
        seam_kernel, [jax.ShapeDtypeStruct(stats.shape, jnp.float32)], stats, edges, halo,
    )
    for mask in (1, 3):
        stats = stats + send(stats, "rng", lambda i: i ^ mask)
    phase, total = kernel_call(
        slope_kernel,
        [
            jax.ShapeDtypeStruct((1, stats.shape[1]), jnp.float32),
            jax.ShapeDtypeStruct((8, LANES), jnp.float32),
        ],
        stats,
        send(stats, "rng", lambda i: i ^ 4),
    )
    before = jnp.zeros_like(total)
    for mask, bit in ((1, 1), (2, 2), (4, 4), (12, 8)):
        got = send(total, "az", lambda i: i ^ mask)
        before = before + jnp.where((me & bit) != 0, got, 0.0)
        total = total + got
    return apply(real, imag, phase, before)


def solution(mesh):
    in_specs = (
        P("az", None, None, "rng"),
        P(),
        P("rng", "az", None),
        P(None, "az", "rng", None),
        P(None, None, "az"),
    )
    out_specs = P("rng", None, "az")
    return jax.shard_map(
        per_device_body, mesh=mesh, in_specs=in_specs, out_specs=out_specs, check_vma=False
    )
```

```python
import jax
import jax.numpy as jnp
from jax import lax
from jax.experimental import pallas as pl
from jax.experimental.pallas import tpu as pltpu
from jax.sharding import PartitionSpec as P


GUARD = 128
LANES = 128
VMEM = pl.BlockSpec(memory_space=pltpu.VMEM)
SMEM = pl.BlockSpec(memory_space=pltpu.SMEM)
HBM = pl.BlockSpec(memory_space=pltpu.HBM)
ANY = pl.BlockSpec(memory_space=pl.ANY)

PIO2_HI = 1.5707964
PIO2_LO = -4.371139e-8


def sine_cosine(x):
    turns = jnp.round(x * 0.63661975)
    r = (x - turns * PIO2_HI) - turns * PIO2_LO
    r2 = r * r
    sine = r + r * r2 * (-1.6666654611e-1 + r2 * (8.3321608736e-3 + r2 * -1.9515295891e-4))
    cosine = 1.0 - 0.5 * r2 + r2 * r2 * (
        4.166664568298827e-2 + r2 * (-1.388731625493765e-3 + r2 * 2.443315711809948e-5)
    )
    quadrant = turns.astype(jnp.int32)
    odd = (quadrant & 1) == 1
    first = jnp.where(odd, cosine, sine)
    second = jnp.where(odd, sine, cosine)
    sine = jnp.where((quadrant & 2) == 2, -first, first)
    cosine = jnp.where(((quadrant + 1) & 2) == 2, -second, second)
    return sine, cosine


def kernel_call(body, out_shape, *args, scalars=0, vmem_mib=8):
    return pl.pallas_call(
        body,
        in_specs=[SMEM] * scalars + [VMEM] * (len(args) - scalars),
        out_specs=[VMEM] * len(out_shape),
        out_shape=out_shape,
        compiler_params=pltpu.CompilerParams(vmem_limit_bytes=vmem_mib << 20),
    )(*args)


def steering_kernel(scale, phase_hbm, re_hbm, im_hbm, edge_hbm, phases, re_ref, im_ref, edge_ref, sems, done):
    pings, hydrophones, cells = phases.shape
    rows = 2 * hydrophones
    for p in range(pings):
        pltpu.make_async_copy(phase_hbm.at[p], phases.at[p], sems.at[p]).start()
    lane = lax.broadcasted_iota(jnp.int32, (rows, LANES), 1)
    for p in range(pings):
        pltpu.make_async_copy(phase_hbm.at[p], phases.at[p], sems.at[p]).wait()
        here = pl.ds(rows * p, rows)
        upper = pl.ds(rows * p, hydrophones)
        lower = pl.ds(rows * p + hydrophones, hydrophones)
        sine, cosine = sine_cosine(phases[p])
        steer_re = (cosine * scale).astype(jnp.bfloat16)
        steer_im = (sine * scale).astype(jnp.bfloat16)
        re_ref[upper] = steer_re
        re_ref[lower] = -steer_im
        im_ref[upper] = steer_im
        im_ref[lower] = steer_re
        pltpu.make_async_copy(re_ref.at[here], re_hbm.at[here], done.at[0]).start()
        pltpu.make_async_copy(im_ref.at[here], im_hbm.at[here], done.at[1]).start()
    for p in range(pings):
        here = pl.ds(rows * p, rows)
        first_re = re_ref[here, :LANES].astype(jnp.float32)
        first_im = pltpu.roll(im_ref[here, :LANES].astype(jnp.float32), 1, 1)
        last_re = pltpu.roll(re_ref[here, cells - LANES :].astype(jnp.float32), LANES - 1, 1)
        last_im = im_ref[here, cells - LANES :].astype(jnp.float32)
        mixed = jnp.where(
            lane < 64,
            jnp.where(lane == 0, first_re, first_im),
            jnp.where(lane == LANES - 1, last_im, last_re),
        )
        edge_ref[:, here] = mixed.T.astype(jnp.bfloat16)
    edge_copy = pltpu.make_async_copy(edge_ref, edge_hbm, done.at[2])
    edge_copy.start()
    pltpu.make_async_copy(re_ref, re_hbm, done.at[0]).wait()
    pltpu.make_async_copy(im_ref, im_hbm, done.at[1]).wait()
    edge_copy.wait()


def steering(phases):
    pings, hydrophones, cells = phases.shape
    rows = pings * 2 * hydrophones
    scale = float(1.0 / (pings * hydrophones) ** 0.5)
    out = jax.ShapeDtypeStruct((rows, cells), jnp.bfloat16)
    edge = jax.ShapeDtypeStruct((LANES, rows), jnp.bfloat16)
    return pl.pallas_call(
        lambda *refs: steering_kernel(scale, *refs),
        in_specs=[HBM],
        out_specs=[HBM] * 3,
        out_shape=[pltpu.HBM(o.shape, o.dtype) for o in (out, out, edge)],
        scratch_shapes=[
            pltpu.VMEM(phases.shape, jnp.float32),
            pltpu.VMEM((rows, cells), jnp.bfloat16),
            pltpu.VMEM((rows, cells), jnp.bfloat16),
            pltpu.VMEM((LANES, rows), jnp.bfloat16),
            pltpu.SemaphoreType.DMA((pings,)),
            pltpu.SemaphoreType.DMA((3,)),
        ],
        compiler_params=pltpu.CompilerParams(vmem_limit_bytes=12 << 20),
        name="steering",
    )(pltpu.with_memory_space_constraint(phases, pltpu.HBM))


def focus_kernel(n_slots, me_ref, owner_ref, start_ref, *refs):
    slots = refs[:n_slots]
    ends = refs[n_slots : n_slots + n_slots // 2]
    interp_ref, weight_hbm, out_ref, edge_ref, window, weight_ref, place_ref, ping_ref, sems = refs[
        n_slots + n_slots // 2 :
    ]
    me = me_ref[0]
    pings, range_cells, band = interp_ref.shape
    rows, width = slots[0].shape
    blocks = start_ref.shape[0]
    cells = range_cells // blocks
    span = band + LANES
    for s in range(n_slots):
        place_ref[s] = -1
    owners = [owner_ref[p] for p in range(pings)]
    relative = [((((o >> 2) - (me >> 2)) & 3) << 2) | ((o ^ me) & 3) for o in owners]
    for p in range(pings):
        k = sum((relative[q] < relative[p]).astype(jnp.int32) for q in range(pings) if q != p)
        place_ref[relative[p]] = k
        ping_ref[k] = p
    for s in range(n_slots):
        k = place_ref[s]
        end = ends[s // 4 * 2 + s % 2].at[s // 2 % 2]

        @pl.when(k >= 0)
        def _():
            for source, low in (
                (slots[s], GUARD),
                (end.at[:, pl.ds(0, GUARD)], 0),
                (end.at[:, pl.ds(GUARD, GUARD)], GUARD + width),
            ):
                part = window.at[k, :, pl.ds(low, source.shape[1])]
                pltpu.make_async_copy(source, part, sems.at[k]).start()

    weight_copy = pltpu.make_async_copy(weight_hbm, weight_ref, sems.at[pings])
    weight_copy.start()
    for k in range(pings):
        pltpu.make_async_copy(window.at[k], window.at[k], sems.at[k]).wait()
        p = ping_ref[k]
        column = pl.ds(pl.multiple_of(p * rows, LANES), rows)
        for b in range(blocks):
            start = start_ref[b, 0, p]
            aligned = jnp.minimum((start // LANES) * LANES, width + 2 * GUARD - span)
            aligned = pl.multiple_of(aligned, LANES)
            wide = window[k, :, pl.ds(aligned, span)]
            slab = pltpu.roll(wide, span - (start - aligned), 1)[:, :band]
            kernel = interp_ref[p, b * cells : (b + 1) * cells, :]
            got = lax.dot_general(
                kernel, slab, (((1,), (1,)), ((), ())), preferred_element_type=jnp.float32
            )
            out_ref[b * cells : (b + 1) * cells, column] = got.astype(jnp.bfloat16)

    weight_copy.wait()
    got = lax.dot_general(
        weight_ref[...], out_ref[...], (((1,), (1,)), ((), ())), preferred_element_type=jnp.float32
    )
    edge_ref[0:2, :] = got[0:2].astype(jnp.bfloat16).astype(jnp.float32)
    edge_ref[2:4, :] = got[LANES - 2 :].astype(jnp.bfloat16).astype(jnp.float32)


def focus(slots, ends, me, owner_map, starts, interp, edge_weights):
    pings, range_cells, _ = interp.shape
    rows, width = slots[0].shape
    call = pl.pallas_call(
        lambda *refs: focus_kernel(len(slots), *refs),
        in_specs=[SMEM] * 3 + [ANY] * (len(slots) + len(ends)) + [VMEM, HBM],
        out_specs=[VMEM] * 2,
        out_shape=[
            jax.ShapeDtypeStruct((range_cells, pings * rows), jnp.bfloat16),
            jax.ShapeDtypeStruct((4, range_cells), jnp.float32),
        ],
        scratch_shapes=[
            pltpu.VMEM((pings, rows, width + 2 * GUARD), jnp.bfloat16),
            pltpu.VMEM(edge_weights.shape, jnp.bfloat16),
            pltpu.SMEM((len(slots),), jnp.int32),
            pltpu.SMEM((pings,), jnp.int32),
            pltpu.SemaphoreType.DMA((pings + 1,)),
        ],
        compiler_params=pltpu.CompilerParams(vmem_limit_bytes=16 << 20),
        name="focus",
    )
    edge_weights = pltpu.with_memory_space_constraint(edge_weights, pltpu.HBM)
    return call(me, owner_map, starts, *slots, *ends, interp, edge_weights)


def image_kernel(focused_ref, re_ref, im_ref, out_re, out_im, stats_ref):
    tile = 512
    rows, cells = out_re.shape
    focused = focused_ref[...]
    for n in range(cells // tile):
        part = slice(n * tile, (n + 1) * tile)
        out_re[:, part] = jnp.dot(
            focused, re_ref[:, part], preferred_element_type=jnp.float32
        ).astype(jnp.bfloat16)
        out_im[:, part] = jnp.dot(
            focused, im_ref[:, part], preferred_element_type=jnp.float32
        ).astype(jnp.bfloat16)
    step = 16
    half = 512

    def fold(x):
        return x[:8] + x[8:]

    stats_ref[...] = jnp.zeros_like(stats_ref)
    for low in range(0, cells, half):
        last = low + half == cells
        span = half if last else half + LANES

        def body(i, carry):
            power, real, imag = carry
            here = pl.ds(pl.multiple_of(i * step, step), step)
            a = out_re[here, low : low + span].astype(jnp.float32)
            b = out_im[here, low : low + span].astype(jnp.float32)
            na = pltpu.roll(a, span - 1, 1)[:, :half]
            nb = pltpu.roll(b, span - 1, 1)[:, :half]
            a, b = a[:, :half], b[:, :half]
            power = power + fold(a * a + b * b)
            real = real + fold(a * na + b * nb)
            imag = imag + fold(a * nb - b * na)
            return power, real, imag

        zero = jnp.zeros((8, half), jnp.float32)
        sums = lax.fori_loop(0, rows // step, body, (zero, zero, zero), unroll=8)
        for k, value in enumerate(sums):
            stats_ref[k : k + 1, low : low + half] = jnp.sum(value, axis=0, keepdims=True)


def image(focused, steer_re, steer_im):
    rows, cells = focused.shape[0], steer_re.shape[1]
    out = jax.ShapeDtypeStruct((rows, cells), jnp.bfloat16)
    return kernel_call(
        image_kernel,
        [out, out, jax.ShapeDtypeStruct((4, cells), jnp.float32)],
        focused,
        steer_re,
        steer_im,
    )


def seam_kernel(stats_ref, edges_ref, halo_ref, out_ref):
    cells = stats_ref.shape[1]
    last_re, last_im = edges_ref[2:3, :], edges_ref[3:4, :]
    next_re, next_im = halo_ref[0:1, :], halo_ref[1:2, :]
    real = jnp.sum(last_re * next_re + last_im * next_im, axis=1, keepdims=True)
    imag = jnp.sum(last_re * next_im - last_im * next_re, axis=1, keepdims=True)
    at = lax.broadcasted_iota(jnp.int32, (1, cells), 1) == cells - 1
    out_ref[...] = stats_ref[...]
    out_ref[1:2, :] = jnp.where(at, real, stats_ref[1:2, :])
    out_ref[2:3, :] = jnp.where(at, imag, stats_ref[2:3, :])


def slope_kernel(stats_ref, more_ref, phase_ref, total_ref):
    cells = stats_ref.shape[1]
    stats = stats_ref[...] + more_ref[...]
    power, real, imag = stats[0:1] + 1e-06, stats[1:2], stats[2:3]
    first = imag / power
    second = (imag * jnp.cos(first) - real * jnp.sin(first)) / power
    slope = first + second
    lane = lax.broadcasted_iota(jnp.int32, (1, cells), 1)
    summed = slope
    step = 1
    while step < cells:
        summed = summed + jnp.where(lane >= step, pltpu.roll(summed, step, 1), 0.0)
        step *= 2
    phase_ref[...] = summed - slope
    total_ref[...] = jnp.broadcast_to(jnp.sum(slope, axis=1, keepdims=True), total_ref.shape)


def apply_kernel(re_ref, im_ref, phase_ref, before_ref, out_ref, scratch, cos_ref, sin_ref):
    tiles = re_ref.shape[1] // LANES
    step = out_ref.shape[0] // (2 * tiles)
    stride = scratch.shape[0] // step

    @pl.when(pl.program_id(0) == 0)
    def _():
        phase = phase_ref[...] + before_ref[0:1, 0:1]
        cos_ref[...] = jnp.cos(phase)
        sin_ref[...] = jnp.sin(phase)

    here = pl.ds(pl.multiple_of(pl.program_id(0) * step, step), step)
    for t in range(tiles):
        part = slice(t * LANES, (t + 1) * LANES)
        a = re_ref[here, part].astype(jnp.float32)
        b = im_ref[here, part].astype(jnp.float32)
        cosine = cos_ref[:, part]
        sine = sin_ref[:, part]
        scratch[pl.ds(2 * t, step, stride=stride), :] = a * cosine + b * sine
        scratch[pl.ds(2 * t + 1, step, stride=stride), :] = b * cosine - a * sine
    for r in range(step):
        cell = scratch[r * stride : r * stride + 2 * tiles, :]
        out_ref[2 * tiles * r : 2 * tiles * (r + 1), :] = cell.astype(jnp.bfloat16)


def apply(real, imag, phase, before):
    rows, cells = real.shape
    tiles = cells // LANES
    step = 128
    out = pl.pallas_call(
        apply_kernel,
        grid=(rows // step,),
        in_specs=[VMEM] * 4,
        out_specs=pl.BlockSpec((step * 2 * tiles, LANES), lambda i: (i, 0)),
        out_shape=jax.ShapeDtypeStruct((rows * 2 * tiles, LANES), jnp.bfloat16),
        scratch_shapes=[
            pltpu.VMEM((step * (2 * tiles + 2), LANES), jnp.float32),
            pltpu.VMEM((1, cells), jnp.float32),
            pltpu.VMEM((1, cells), jnp.float32),
        ],
        compiler_params=pltpu.CompilerParams(vmem_limit_bytes=12 << 20),
        name="apply",
    )(real, imag, phase, before)
    out = out.reshape(rows, tiles, 2, LANES).transpose(0, 2, 1, 3)
    return out.reshape(rows, 2, cells)


def send(x, axis, move):
    n = lax.axis_size(axis)
    return lax.ppermute(x, axis, [(i, move(i)) for i in range(n)])


def up(x):
    return send(x, "az", lambda i: (i + 4) % 16)


def down(x):
    return send(x, "az", lambda i: (i - 4) % 16)


def across(x):
    return send(x, "az", lambda i: i ^ 2)


def partner(x):
    return send(x, "az", lambda i: i ^ 1)


def spread(block):
    n = lax.axis_size("rng")
    width = block.shape[1]
    above, below, other = up(block), down(block), across(block)
    low = lax.ppermute(block[:, width - GUARD :], "rng", [(i, i + 1) for i in range(n - 1)])
    high = lax.ppermute(block[:, :GUARD], "rng", [(i + 1, i) for i in range(n - 1)])
    ends = jnp.concatenate([low, high], axis=1)
    passed = jnp.where(lax.axis_index("az") & 1 == 0, above, below)
    opposite = send(passed, "az", lambda i: (i + (4, -4)[i & 1]) % 16)
    slots = {(0, 0): block, (3, 0): above, (1, 0): below, (2, 0): opposite, (0, 1): other}
    slots[3, 1] = up(other)
    slots[1, 1] = down(other)
    slots[2, 1] = across(opposite)
    ends = jnp.stack([ends, across(ends)])
    far = send(ends, "az", lambda i: (i + 8) % 16)
    ends = [ends, down(ends), far, up(ends)]
    out_slots, out_ends = [], []
    for y in range(4):
        out_ends += [ends[y], partner(ends[y])]
        for z in range(2):
            out_slots += [slots[y, z], partner(slots[y, z])]
    return out_slots, out_ends


def per_device_body(echoes, owner_map, band_start, interp, steer_phase):
    hydrophones, samples = echoes.shape[2:]
    n_az = lax.axis_size("az")
    me = lax.axis_index("az")
    steer_re, steer_im, edge_weights = steering(steer_phase)
    slots, ends = spread(echoes[0].reshape(2 * hydrophones, samples))
    focused, edges = focus(
        slots, ends, me.reshape(1), owner_map, band_start, interp[:, 0], edge_weights
    )
    halo = lax.ppermute(edges[:2], "az", [(i + 1, i) for i in range(n_az - 1)])
    real, imag, stats = image(focused, steer_re, steer_im)
    (stats,) = kernel_call(
        seam_kernel, [jax.ShapeDtypeStruct(stats.shape, jnp.float32)], stats, edges, halo,
    )
    for mask in (1, 3):
        stats = stats + send(stats, "rng", lambda i: i ^ mask)
    phase, total = kernel_call(
        slope_kernel,
        [
            jax.ShapeDtypeStruct((1, stats.shape[1]), jnp.float32),
            jax.ShapeDtypeStruct((8, LANES), jnp.float32),
        ],
        stats,
        send(stats, "rng", lambda i: i ^ 4),
    )
    before = jnp.zeros_like(total)
    for mask, bit in ((1, 1), (2, 2), (4, 4), (12, 8)):
        got = send(total, "az", lambda i: i ^ mask)
        before = before + jnp.where((me & bit) != 0, got, 0.0)
        total = total + got
    return apply(real, imag, phase, before)


def solution(mesh):
    in_specs = (
        P("az", None, None, "rng"),
        P(),
        P("rng", "az", None),
        P(None, "az", "rng", None),
        P(None, None, "az"),
    )
    out_specs = P("rng", None, "az")
    return jax.shard_map(
        per_device_body, mesh=mesh, in_specs=in_specs, out_specs=out_specs, check_vma=False
    )
```
